32 devices in a mesh: rep: 2 (over y), gx: 16 (over z, x, core).
Axes of the slice: x: 2, y: 2, z: 4, core: 2. Of those that a mesh axis runs over, the one named last changes fastest.
Arguments:
- positions: float32 [3, 32768], P(None, ('rep', 'gx')), parts along dimension 1, may hold values from 0 to 8, as said below
- field: float32 [3, 32768], P(None, ('rep', 'gx')), parts along dimension 1, may hold values from -45 to 45
- inv_polar: float32 [32768], P(('rep', 'gx')), parts along dimension 0, may hold values from 2 to 8
- x_spline: float32 [2, 5, 32768], P(None, None, ('rep', 'gx')), parts along dimension 2, may hold values from -1 to 1, as said below
- yz_spline: float32 [4, 32768, 128], P(None, ('rep', 'gx')), parts along dimension 1, may hold values from -1 to 1, as said below
- tile_list: int32 [256, 7], P(('rep', 'gx')), parts along dimension 0, may hold values from 0 to 13, as said below
- tile_count: int32 [256], P(('rep', 'gx')), parts along dimension 0, may hold values from 1 to 7, as said below
Outputs:
- dipoles: float32 [3, 32768], P(None, ('rep', 'gx')), parts along dimension 1
- residual: float32 [3, 32768], P(None, ('rep', 'gx')), parts along dimension 1
The draws below stay inside these ranges and needn't reach their ends.
There are 2 independent parts, one for each index of `rep`. The reference program is written for one: setup_inputs(seed, part) draws one part's arguments, and reference() takes and returns one part's arrays. A program takes and returns all parts, laid end to end along the dimension named above; each array names one. Nothing has to cross between parts.
Inputs may be any that keep to these rules, and one draw needn't show every extreme that they name: `positions`: the first coordinate of an atom of block b of its slab lies in [b, b + 1); the other two lie in [0, 2). x_spline[0, k, i] and x_spline[1, k, i] are the cardinal B-spline of order 5 and its derivative at u_i + 4 - k for some u_i in [0, 1). `yz_spline`: rows 0 and 1 hold, for each atom, the cardinal B-spline of order 5 and its derivative at u + 4 - k placed at grid line (t + k) mod 128 for k < 5, for some start t and some u in [0, 1), and zero elsewhere; rows 2 and 3 likewise with their own start and offset. `tile_list`: row g = s * 8 + b lists in rising order the extended blocks b + 3 + e, -3 <= e <= 3, for which global blocks g and g + e (modulo 128) are neighbours; being neighbours is symmetric and always holds for e = 0; entries from tile_count[g] on equal b + 3. `tile_count`: global block 0 has all 7 neighbours.
All inputs are finite; a program needn't handle non-finite values.
Results may differ from the reference program's by a relative error of at most 0.0003.
Values sent between devices are 32-bit elements; how exact they have to be, the bound alone decides.
A program may use at most 64 MiB of HBM per device.

```python
import math
import jax
import jax.numpy as jnp
from jax import lax

GRID = 128
ORDER = 5
TILE = 128
HALO_BLK = 3
ITERS = 3
ATOM_DEV = 1024
NNB = 7
ATOMS = 16384
SLAB_BLOCKS = 8
BLOCKS = 128
N_GX = 16


def cardinal(order_now, at_point):
    if order_now == 2:
        return jnp.maximum(0.0, 1.0 - jnp.abs(at_point - 1.0))
    lower_part = cardinal(order_now - 1, at_point)
    upper_part = cardinal(order_now - 1, at_point - 1.0)
    return (at_point * lower_part + (order_now - at_point) * upper_part) / (order_now - 1)


def spline_pair(frac):
    shifts = (ORDER - 1 - jnp.arange(ORDER, dtype=jnp.int32)).astype(jnp.float32)
    points = frac[None, :] + shifts[:, None]
    spline_value = cardinal(ORDER, points)
    spline_slope = cardinal(ORDER - 1, points) - cardinal(ORDER - 1, points - 1.0)
    return (spline_value, spline_slope)


def draw_positions(key, part):
    atom_index = jnp.arange(ATOMS, dtype=jnp.int32)
    block_of = (atom_index % ATOM_DEV // TILE).astype(jnp.float32)
    uniform_draw = jax.random.uniform(key, (3, ATOMS), jnp.float32)
    return jnp.stack([block_of + uniform_draw[0], 2.0 * uniform_draw[1], 2.0 * uniform_draw[2]]).astype(jnp.float32)


def draw_field(key, part):
    atom_index = jnp.arange(ATOMS, dtype=jnp.int32)
    slab_of = (atom_index // ATOM_DEV).astype(jnp.float32)
    slab_total = ATOMS // ATOM_DEV
    ramp = 1.0 + 2.0 * slab_of / max(slab_total - 1, 1)
    normal_draw = jnp.clip(jax.random.normal(jax.random.fold_in(key, 1), (3, ATOMS), jnp.float32), -4.0, 4.0)
    return (normal_draw * ramp[None, :]).astype(jnp.float32)


def draw_x_spline(key, part):
    frac = jax.random.uniform(key, (ATOMS,), jnp.float32)
    spline_value, spline_slope = spline_pair(frac)
    return jnp.stack([spline_value, spline_slope]).astype(jnp.float32)


def draw_yz_spline(key, part):
    grid_lines = jnp.arange(GRID, dtype=jnp.int32)
    tables = []
    for axis_code in (1, 2):
        sub_key = jax.random.fold_in(key, axis_code)
        start_line = jax.random.randint(jax.random.fold_in(sub_key, 1), (ATOMS,), 0, GRID, dtype=jnp.int32)
        frac = jax.random.uniform(jax.random.fold_in(sub_key, 2), (ATOMS,), jnp.float32)
        spline_value, spline_slope = spline_pair(frac)
        dense_value = jnp.zeros((ATOMS, GRID), jnp.float32)
        dense_slope = jnp.zeros((ATOMS, GRID), jnp.float32)
        for spline_step in range(ORDER):
            matches = ((start_line + spline_step) % GRID)[:, None] == grid_lines[None, :]
            dense_value = dense_value + jnp.where(matches, spline_value[spline_step][:, None], 0.0)
            dense_slope = dense_slope + jnp.where(matches, spline_slope[spline_step][:, None], 0.0)
        tables.append(dense_value)
        tables.append(dense_slope)
    return jnp.stack(tables).astype(jnp.float32)


def neighbour_table(key):
    block_ids = jnp.arange(BLOCKS, dtype=jnp.int32)
    reach = jnp.arange(1, HALO_BLK + 1, dtype=jnp.int32)
    coins = jax.random.randint(jax.random.fold_in(key, 7), (BLOCKS, HALO_BLK), 0, 2, dtype=jnp.int32)
    first_block = block_ids == 0
    partner = (block_ids[:, None] + reach[None, :]) % BLOCKS
    coins = jnp.where(first_block[:, None] | first_block[partner], 1, coins)
    upper_side = coins
    lower_rows = (block_ids[:, None] - reach[None, :]) % BLOCKS
    lower_side = coins[lower_rows, (reach - 1)[None, :]]
    linked = jnp.concatenate([lower_side[:, ::-1], jnp.ones((BLOCKS, 1), jnp.int32), upper_side], axis=1)
    live_count = jnp.sum(linked, axis=1).astype(jnp.int32)
    slot_ids = jnp.arange(NNB, dtype=jnp.int32)
    sort_keys = jnp.where(linked == 1, slot_ids[None, :], NNB + slot_ids[None, :])
    ordering = jnp.argsort(sort_keys, axis=1, stable=True).astype(jnp.int32)
    local_block = (block_ids % SLAB_BLOCKS)[:, None]
    entries = jnp.where(slot_ids[None, :] < live_count[:, None], local_block + ordering, local_block + HALO_BLK)
    return (entries.astype(jnp.int32), live_count)


def draw_tile_list(key, part):
    entries, live_count = neighbour_table(key)
    return entries


def draw_tile_count(key, part):
    entries, live_count = neighbour_table(key)
    return live_count.astype(jnp.int32)


def levels(stream_key, shape, split, low, high):
    gain, own = 1.0, jax.random.fold_in(stream_key, 6)
    for dim, shards_of in split:
        draws = jnp.exp(jax.random.uniform(jax.random.fold_in(own, dim), (shards_of,), jnp.float32, low / len(split), high / len(split)))
        gain = gain * jnp.repeat(draws, shape[dim] // shards_of).reshape([-1 if axis == dim else 1 for axis in range(len(shape))])
    return gain


def setup_inputs(seed: int = 0, part: int = 0) -> dict:
    keys = jax.random.split(jax.random.key(seed), 8)
    part_keys = jax.random.split(jax.random.fold_in(keys[7], part), 8)
    positions = draw_positions(jax.random.fold_in(jax.random.fold_in(keys[7], part), 71), part)
    field = draw_field(jax.random.fold_in(jax.random.fold_in(keys[7], part), 71), part)
    inv_polar = jnp.clip(jnp.exp(math.log(8.0) - 1.3862944 * jax.random.uniform(part_keys[2], (ATOMS,), jnp.float32) ** levels(part_keys[2], (ATOMS,), ((0, 16),), -0.2, 0.2)), 2.0, 8.0)
    x_spline = draw_x_spline(jax.random.fold_in(jax.random.fold_in(keys[7], part), 71), part)
    yz_spline = draw_yz_spline(jax.random.fold_in(jax.random.fold_in(keys[7], part), 71), part)
    tile_list = draw_tile_list(jax.random.fold_in(jax.random.fold_in(keys[7], part), 71), part)
    tile_count = draw_tile_count(jax.random.fold_in(jax.random.fold_in(keys[7], part), 71), part)
    return {"positions": positions, "field": field, "inv_polar": inv_polar, "x_spline": x_spline, "yz_spline": yz_spline, "tile_list": tile_list, "tile_count": tile_count}


PAIR_C = 0.025
RECIP_C = 8192.0
DAMP = 0.0008
EXACT = lax.Precision.HIGHEST

def pair_field(home_pos, ext_pos, ext_vec, tile_rows, live_counts):
    slab_blocks = home_pos.shape[1] // TILE
    ext_blocks = ext_pos.shape[1] // TILE
    home_blocks = home_pos.reshape(3, slab_blocks, TILE).transpose(1, 0, 2)
    pos_blocks = ext_pos.reshape(3, ext_blocks, TILE)
    vec_blocks = ext_vec.reshape(3, ext_blocks, TILE)
    slot_index = jnp.arange(tile_rows.shape[1], dtype=jnp.int32)
    self_pair = jnp.eye(TILE, dtype=bool)

    def one_block(carried, scan_item):
        home_block, tile_row, live_count, block_index = scan_item
        near_pos = jnp.take(pos_blocks, tile_row, axis=1)
        near_vec = jnp.take(vec_blocks, tile_row, axis=1)
        offsets = home_block[:, None, :, None] - near_pos[:, :, None, :]
        distance_sq = lax.optimization_barrier(jnp.sum(offsets * offsets, axis=0)) + 1.0
        inverse = lax.rsqrt(distance_sq)
        third_power = inverse * inverse * inverse
        fifth_power = third_power * inverse * inverse
        same_block = (tile_row == block_index + HALO_BLK)[:, None, None]
        live_mask = (slot_index < live_count)[:, None, None] & ~(same_block & self_pair[None])
        third_power = jnp.where(live_mask, third_power, 0.0)
        fifth_power = jnp.where(live_mask, fifth_power, 0.0)
        projection = lax.optimization_barrier(jnp.sum(offsets * near_vec[:, :, None, :], axis=0))
        field_sum = lax.optimization_barrier(jnp.sum(third_power[None] * near_vec[:, :, None, :] - 3.0 * (fifth_power * projection)[None] * offsets, axis=(1, 3)))
        return (carried, PAIR_C * field_sum)
    block_ids = jnp.arange(slab_blocks, dtype=jnp.int32)
    unused_carry, blocks_out = lax.scan(one_block, jnp.zeros((), jnp.float32), (home_blocks, tile_rows, live_counts, block_ids))
    return blocks_out.transpose(1, 0, 2).reshape(3, slab_blocks * TILE)

def slab_weights(local_plane, x_spline, planes):
    spline_steps = jnp.arange(ORDER, dtype=jnp.int32)
    plane_index = jnp.arange(planes, dtype=jnp.int32)
    matches = local_plane[None, :, None] + spline_steps[:, None, None] == plane_index[None, None, :]
    spline_value = lax.optimization_barrier(jnp.sum(jnp.where(matches, x_spline[0][:, :, None], 0.0), axis=0))
    spline_slope = lax.optimization_barrier(jnp.sum(jnp.where(matches, x_spline[1][:, :, None], 0.0), axis=0))
    return (spline_value, spline_slope)

def spread_dipoles(vector, spline_value, spline_slope, yz_spline):
    atoms_here = spline_value.shape[0]
    planes = spline_value.shape[1]
    grid_lines = yz_spline.shape[2]
    lead_terms = (vector[0][:, None] * spline_slope)[:, :, None] * yz_spline[0][:, None, :]
    lead_terms = lead_terms + (vector[1][:, None] * spline_value)[:, :, None] * yz_spline[1][:, None, :]
    tail_terms = (vector[2][:, None] * spline_value)[:, :, None] * yz_spline[0][:, None, :]
    contract = (((0,), (0,)), ((), ()))
    charge = lax.dot_general(lead_terms.reshape(atoms_here, planes * grid_lines), yz_spline[2], contract, precision=EXACT)
    charge = charge + lax.dot_general(tail_terms.reshape(atoms_here, planes * grid_lines), yz_spline[3], contract, precision=EXACT)
    return charge.reshape(planes, grid_lines, grid_lines)

def gather_field(potential, spline_value, spline_slope, yz_spline):
    planes = potential.shape[0]
    grid_lines = potential.shape[1]
    atoms_here = spline_value.shape[0]
    flat_grid = potential.reshape(planes * grid_lines, grid_lines)
    contract = (((1,), (1,)), ((), ()))
    plain_sum = lax.dot_general(yz_spline[2], flat_grid, contract, precision=EXACT).reshape(atoms_here, planes, grid_lines)
    tilted_sum = lax.dot_general(yz_spline[3], flat_grid, contract, precision=EXACT).reshape(atoms_here, planes, grid_lines)
    first_comp = lax.optimization_barrier(jnp.sum(spline_slope[:, :, None] * yz_spline[0][:, None, :] * plain_sum, axis=(1, 2)))
    second_comp = lax.optimization_barrier(jnp.sum(spline_value[:, :, None] * yz_spline[1][:, None, :] * plain_sum, axis=(1, 2)))
    third_comp = lax.optimization_barrier(jnp.sum(spline_value[:, :, None] * yz_spline[0][:, None, :] * tilted_sum, axis=(1, 2)))
    return jnp.stack([first_comp, second_comp, third_comp])

def reference_kernel():
    freq = jnp.arange(GRID, dtype=jnp.int32)
    signed = jnp.where(freq <= GRID // 2, freq, freq - GRID).astype(jnp.float32)
    last_freq = jnp.arange(GRID // 2 + 1, dtype=jnp.int32).astype(jnp.float32)
    mode_sq = signed[:, None, None] * signed[:, None, None] + signed[None, :, None] * signed[None, :, None] + last_freq[None, None, :] * last_freq[None, None, :]
    safe_sq = jnp.where(mode_sq > 0, mode_sq, 1.0)
    return jnp.where(mode_sq > 0, RECIP_C * jnp.exp(-DAMP * safe_sq) / safe_sq, 0.0)

def reference(positions, field, inv_polar, x_spline, yz_spline, tile_list, tile_count):
    slabs = N_GX
    planes = GRID // slabs
    extent = planes + 4
    halo_atoms = HALO_BLK * TILE
    slab_blocks = ATOM_DEV // TILE
    slab_ids = jnp.arange(slabs, dtype=jnp.int32)
    shift_x = jnp.concatenate([jnp.full((halo_atoms,), -1.0 * slab_blocks, jnp.float32), jnp.zeros((ATOM_DEV,), jnp.float32), jnp.full((halo_atoms,), 1.0 * slab_blocks, jnp.float32)])
    kernel = reference_kernel()
    place = slab_ids[:, None] * planes + jnp.arange(extent, dtype=jnp.int32)[None, :]
    local_plane = (jnp.arange(ATOM_DEV, dtype=jnp.int32) * planes // ATOM_DEV).astype(jnp.int32)

    def wrap_pad(array):
        return jnp.concatenate([array[:, -halo_atoms:], array, array[:, :halo_atoms]], axis=1)
    pos_pad = wrap_pad(positions)

    def slab_parts(slab):
        begin = slab * ATOM_DEV
        own_pos = lax.dynamic_slice_in_dim(positions, begin, ATOM_DEV, 1)
        ext_pos = lax.dynamic_slice_in_dim(pos_pad, begin, ATOM_DEV + 2 * halo_atoms, 1)
        ext_pos = ext_pos.at[0].add(shift_x)
        splines = lax.dynamic_slice_in_dim(x_spline, begin, ATOM_DEV, 2)
        dense = lax.dynamic_slice_in_dim(yz_spline, begin, ATOM_DEV, 1)
        tile_rows = lax.dynamic_slice_in_dim(tile_list, slab * slab_blocks, slab_blocks, 0)
        live_counts = lax.dynamic_slice_in_dim(tile_count, slab * slab_blocks, slab_blocks, 0)
        spline_value, spline_slope = slab_weights(local_plane, splines, extent)
        return (own_pos, ext_pos, spline_value, spline_slope, dense, tile_rows, live_counts)

    def apply(vector):
        vec_pad = wrap_pad(vector)

        def near_and_charge(slab):
            parts = slab_parts(slab)
            begin = slab * ATOM_DEV
            ext_vec = lax.dynamic_slice_in_dim(vec_pad, begin, ATOM_DEV + 2 * halo_atoms, 1)
            own_vec = lax.dynamic_slice_in_dim(vector, begin, ATOM_DEV, 1)
            near_field = pair_field(parts[0], parts[1], ext_vec, parts[5], parts[6])
            charge = spread_dipoles(own_vec, parts[2], parts[3], parts[4])
            return (near_field, charge)
        near_all, charges = lax.map(near_and_charge, slab_ids)
        padded = jnp.zeros((GRID + 4, GRID, GRID), jnp.float32).at[place].add(charges)
        whole = padded[2:GRID + 2]
        whole = whole.at[GRID - 2:].add(padded[:2]).at[:2].add(padded[GRID + 2:])
        potential = jnp.fft.irfftn(jnp.fft.rfftn(whole) * kernel, s=whole.shape)
        pot_pad = jnp.concatenate([potential[GRID - 2:], potential, potential[:2]], axis=0)

        def far_part(scan_item):
            slab, local_pot = scan_item
            parts = slab_parts(slab)
            return gather_field(local_pot, parts[2], parts[3], parts[4])
        far_all = lax.map(far_part, (slab_ids, pot_pad[place]))
        near_whole = near_all.transpose(1, 0, 2).reshape(3, ATOMS)
        far_whole = far_all.transpose(1, 0, 2).reshape(3, ATOMS)
        return inv_polar[None, :] * vector + far_whole - near_whole
    dipoles = jnp.zeros_like(field)
    residual = field
    precond = field / inv_polar[None, :]
    direction = precond
    rz_now = jnp.sum(residual * precond)
    for sweep_index in range(ITERS):
        applied = apply(direction)
        step_size = rz_now / jnp.sum(direction * applied)
        dipoles = dipoles + step_size * direction
        residual = residual - step_size * applied
        if sweep_index + 1 < ITERS:
            precond = residual / inv_polar[None, :]
            rz_next = jnp.sum(residual * precond)
            direction = precond + rz_next / rz_now * direction
            rz_now = rz_next
    return (dipoles, residual)
```

```python
import jax
import jax.numpy as jnp
from jax import lax
from jax.experimental import pallas as pl
from jax.experimental.pallas import tpu as pltpu
from jax.sharding import PartitionSpec as P
import functools

GRID = 128
ORDER = 5
TILE = 128
HALO_BLK = 3
ITERS = 3


PAIR_C = 0.025
RECIP_C = 8192.0
DAMP = 0.0008
EXACT = lax.Precision.HIGHEST


def mode_of(freq, size):
    half_size = size // 2
    mode_num = jnp.where(freq <= half_size, freq, freq - half_size)
    weight = jnp.where((freq == 0) | (freq == half_size), 1.0 / size, 2.0 / size)
    return (mode_num.astype(jnp.float32), weight.astype(jnp.float32))


def basis_rows(size, points):
    freq = jnp.arange(size, dtype=jnp.int32)
    half_size = size // 2
    mode_num = jnp.where(freq <= half_size, freq, freq - half_size)
    phase = mode_num[:, None] * points[None, :] % size
    angle = phase.astype(jnp.float32) * (2.0 * jnp.pi / size)
    return jnp.where((freq <= half_size)[:, None], jnp.cos(angle), jnp.sin(angle))


def kernel_block(x_modes, x_weights, y_modes, y_weights, z_modes, z_weights):
    mode_sq = (
        x_modes[:, None, None] * x_modes[:, None, None]
        + y_modes[None, :, None] * y_modes[None, :, None]
        + z_modes[None, None, :] * z_modes[None, None, :]
    )
    safe_sq = jnp.where(mode_sq > 0, mode_sq, 1.0)
    green = jnp.where(mode_sq > 0, RECIP_C * jnp.exp(-DAMP * safe_sq) / safe_sq, 0.0)
    return green * x_weights[:, None, None] * y_weights[None, :, None] * z_weights[None, None, :]


F32 = jnp.float32
BF16 = jnp.bfloat16
VMEM = pl.BlockSpec(memory_space=pltpu.VMEM)


def split(x):
    high = x.astype(BF16)
    return high, (x - high.astype(F32)).astype(BF16)


def dot(a, b):
    return jnp.dot(a, b, preferred_element_type=F32)


def params(**more):
    return pltpu.CompilerParams(vmem_limit_bytes=56 * 1024 * 1024, **more)


def prep_kernel(yz_ref, rows_ref, yft_ref, zf_ref, zft_ref):
    rows = rows_ref[...]
    contract = (((1,), (1,)), ((), ()))
    for t in range(2):
        yft_ref[0, t] = lax.dot_general(
            rows, yz_ref[t], contract, precision=EXACT, preferred_element_type=F32
        )
    both = jnp.concatenate([yz_ref[2], yz_ref[3]], axis=0)
    high, low = split(
        lax.dot_general(both, rows, contract, precision=EXACT, preferred_element_type=F32)
    )
    zf_ref[0] = jnp.concatenate([high, low], axis=1)
    high, low = split(
        lax.dot_general(rows, both, contract, precision=EXACT, preferred_element_type=F32)
    )
    zft_ref[0] = jnp.concatenate([high, low], axis=0)


def prepare(yz_spline, rows, blocks):
    return pl.pallas_call(
        prep_kernel,
        grid=(blocks,),
        in_specs=[
            pl.BlockSpec((4, TILE, GRID), lambda b: (0, b, 0)),
            pl.BlockSpec((GRID, GRID), lambda b: (0, 0)),
        ],
        out_specs=[
            pl.BlockSpec((1, 2, GRID, TILE), lambda b: (b, 0, 0, 0)),
            pl.BlockSpec((1, 2 * TILE, 2 * GRID), lambda b: (b, 0, 0)),
            pl.BlockSpec((1, 2 * GRID, 2 * TILE), lambda b: (b, 0, 0)),
        ],
        out_shape=[
            jax.ShapeDtypeStruct((blocks, 2, GRID, TILE), F32),
            jax.ShapeDtypeStruct((blocks, 2 * TILE, 2 * GRID), BF16),
            jax.ShapeDtypeStruct((blocks, 2 * GRID, 2 * TILE), BF16),
        ],
        compiler_params=params(),
        name="prep",
    )(yz_spline, rows)


def spread_kernel(planes, ky_count, pv_ref, xs_ref, yft_ref, zf_ref, out_ref):
    blocks = pv_ref.shape[0]
    ranks = out_ref.shape[0]
    out_ref[...] = jnp.zeros_like(out_ref)

    def one_block(b, carry):
        base = b * planes // blocks
        y, dy = yft_ref[b, 0], yft_ref[b, 1]
        v0, v1, v2 = (pv_ref[b, 3 + c : 4 + c, :] for c in range(3))
        highs, lows = [], []
        for k in range(ORDER):
            x, dx = xs_ref[b, k : k + 1, :], xs_ref[b, ORDER + k : ORDER + k + 1, :]
            lead = (v0 * dx) * y + (v1 * x) * dy
            high, low = split(jnp.concatenate([lead, (v2 * x) * y], axis=1))
            highs.append(high)
            lows.append(low)
        weights = zf_ref[b]
        wide = dot(jnp.concatenate(highs, axis=0), weights)
        total = (
            wide[:, :GRID] + wide[:, GRID:] + dot(jnp.concatenate(lows, axis=0), weights[:, :GRID])
        )
        for k in range(ORDER):
            part = total[k * GRID : (k + 1) * GRID].reshape(ranks, ky_count, GRID)
            out_ref[:, base + k, :ky_count, :] += part
        return carry

    lax.fori_loop(0, blocks, one_block, 0)


def gather_kernel(planes, ky_count, ret_ref, xs_ref, yft_ref, zft_ref, out_ref, wide_ref, low_ref):
    blocks = xs_ref.shape[0]
    extent = ret_ref.shape[1]
    for p in range(extent):
        high, low = split(ret_ref[:, p, :ky_count, :].reshape(GRID, GRID))
        wide_ref[p] = jnp.concatenate([high, high], axis=1)
        low_ref[p] = low

    def one_block(b, carry):
        base = b * planes // blocks
        weights = zft_ref[b]
        wide = wide_ref[pl.ds(base, ORDER)].reshape(ORDER * GRID, 2 * GRID)
        low = low_ref[pl.ds(base, ORDER)].reshape(ORDER * GRID, GRID)
        sums = dot(wide, weights) + dot(low, weights[:GRID])
        one = two = three = 0.0
        for k in range(ORDER):
            x, dx = xs_ref[b, k : k + 1, :], xs_ref[b, ORDER + k : ORDER + k + 1, :]
            plain = sums[k * GRID : (k + 1) * GRID, :TILE]
            one += dx * plain
            two += x * plain
            three += x * sums[k * GRID : (k + 1) * GRID, TILE:]
        y, dy = yft_ref[b, 0], yft_ref[b, 1]
        out_ref[b, 0:1] = jnp.sum(y * one, axis=0, keepdims=True)
        out_ref[b, 1:2] = jnp.sum(dy * two, axis=0, keepdims=True)
        out_ref[b, 2:3] = jnp.sum(y * three, axis=0, keepdims=True)
        return carry

    lax.fori_loop(0, blocks, one_block, 0)


def pair_kernel(near_ref, pv_ref, before_ref, after_ref, out_ref, ext_ref, col_ref, acc_ref):
    blocks = pv_ref.shape[0]
    ext_blocks = ext_ref.shape[0]
    reach = 2 * HALO_BLK + 1
    first_row = lax.broadcasted_iota(jnp.int32, (HALO_BLK, 8, TILE), 1) == 0
    ext_ref[:HALO_BLK] = before_ref[...] + jnp.where(first_row, -1.0 * blocks, 0.0)
    ext_ref[HALO_BLK : HALO_BLK + blocks] = pv_ref[...]
    ext_ref[HALO_BLK + blocks :] = after_ref[...] + jnp.where(first_row, 1.0 * blocks, 0.0)
    acc_ref[...] = jnp.zeros_like(acc_ref)
    lag = lax.broadcasted_iota(jnp.int32, (8, TILE), 1) - lax.broadcasted_iota(
        jnp.int32, (8, TILE), 0
    )

    def one_source(e, carry):
        for c in range(6):
            col_ref[c] = jnp.broadcast_to(ext_ref[e, c : c + 1, :], (TILE, TILE)).T

        def one_home(b, inner):
            @pl.when(near_ref[b * reach + e - b] > 0)
            def _():
                home = [jnp.broadcast_to(pv_ref[b, c : c + 1, :], (8, TILE)) for c in range(3)]
                shift = jnp.where(e == b + HALO_BLK, 0, 4 * TILE)
                direct = [jnp.zeros((8, TILE), F32) for c in range(3)]
                tilted = [jnp.zeros((8, TILE), F32) for c in range(3)]
                for j in range(TILE // 8):
                    rows = slice(8 * j, 8 * j + 8)
                    r = [home[c] - col_ref[c, rows, :] for c in range(3)]
                    v = [col_ref[3 + c, rows, :] for c in range(3)]
                    inverse = lax.rsqrt(r[0] * r[0] + r[1] * r[1] + r[2] * r[2] + 1.0)
                    inverse = jnp.where(lag != 8 * j + shift, inverse, 0.0)
                    square = inverse * inverse
                    third = square * inverse
                    weight = third * square * (r[0] * v[0] + r[1] * v[1] + r[2] * v[2])
                    for c in range(3):
                        direct[c] += third * v[c]
                        tilted[c] += weight * r[c]
                for c in range(3):
                    acc_ref[b, c] += direct[c] - 3.0 * tilted[c]

            return inner

        lo = jnp.maximum(e - (reach - 1), 0)
        hi = jnp.minimum(e + 1, blocks)
        lax.fori_loop(lo, hi, one_home, 0)
        return carry

    lax.fori_loop(0, ext_blocks, one_source, 0)
    for b in range(blocks):
        for c in range(3):
            out_ref[b, c : c + 1] = PAIR_C * jnp.sum(acc_ref[b, c], axis=0, keepdims=True)


def greet(ranks, me):
    barrier = pltpu.get_barrier_semaphore()

    def signal(d, carry):
        pl.semaphore_signal(
            barrier,
            inc=1,
            device_id={"gx": lax.rem(me + d, ranks)},
            device_id_type=pl.DeviceIdType.MESH,
        )
        return carry

    lax.fori_loop(1, ranks, signal, 0)
    pl.semaphore_wait(barrier, ranks - 1)


def exchange(ranks, me, source, target, local_sem, send_sem, recv_sem):
    def copy(d, slot):
        peer = lax.rem(me + d, ranks)
        return pltpu.make_async_remote_copy(
            src_ref=source(peer),
            dst_ref=target(slot),
            send_sem=send_sem.at[d],
            recv_sem=recv_sem.at[d],
            device_id={"gx": peer},
            device_id_type=pl.DeviceIdType.MESH,
        )

    def start(d, carry):
        copy(d, me).start()
        return carry

    def finish(d, carry):
        copy(d, lax.rem(me - d + ranks, ranks)).wait()
        return carry

    lax.fori_loop(1, ranks, start, 0)
    own = pltpu.make_async_copy(source(me), target(me), local_sem)
    own.start()

    def wait():
        own.wait()
        lax.fori_loop(1, ranks, finish, 0)

    return wait


def middle_kernel(
    ranks, ky_count, spec_ref, pv_ref, green_ref, across_ref, back_ref,
    ret_ref, before_ref, after_ref,
    recv_ref, done_ref, local_sems, send1, recv1, send2, recv2, halo_send, halo_recv,
):
    me = lax.axis_index("gx")
    blocks = pv_ref.shape[0]
    extent = spec_ref.shape[1]
    rows = ranks * extent
    greet(ranks, me)
    halos = []
    for t, (piece, into, step) in enumerate(
        (
            (pv_ref.at[pl.ds(blocks - HALO_BLK, HALO_BLK)], before_ref, 1),
            (pv_ref.at[pl.ds(0, HALO_BLK)], after_ref, ranks - 1),
        )
    ):
        halos.append(
            pltpu.make_async_remote_copy(
                src_ref=piece,
                dst_ref=into,
                send_sem=halo_send.at[t],
                recv_sem=halo_recv.at[t],
                device_id={"gx": lax.rem(me + step, ranks)},
                device_id_type=pl.DeviceIdType.MESH,
            )
        )
        halos[-1].start()
    wait = exchange(
        ranks, me, lambda d: spec_ref.at[d], lambda d: recv_ref.at[d], local_sems.at[0], send1, recv1
    )
    across_high, across_low = split(across_ref[...])
    back_high, back_low = split(back_ref[...])
    wait()
    lines_in = recv_ref.reshape(rows * 8, GRID)
    lines_out = done_ref.reshape(rows * 8, GRID)
    for q in range(ky_count):
        high, low = split(lines_in[pl.ds(q, rows, stride=8), :])
        wide = dot(across_high, jnp.concatenate([high, low], axis=1))
        line = wide[:, :GRID] + wide[:, GRID:] + dot(across_low, high)
        high, low = split(line * green_ref[q])
        wide = dot(back_high, jnp.concatenate([high, low], axis=1))
        lines_out[pl.ds(q, rows, stride=8), :] = (
            wide[:, :GRID] + wide[:, GRID:] + dot(back_low, high)
        )
    wait = exchange(
        ranks, me, lambda d: done_ref.at[d], lambda d: ret_ref.at[d], local_sems.at[1], send2, recv2
    )
    for halo in halos:
        halo.wait()
    wait()


def middle(spec, pv, green, across, back, ranks, ky_count):
    dma = pltpu.SemaphoreType.DMA
    halo = jax.ShapeDtypeStruct((HALO_BLK, 8, TILE), F32)
    return pl.pallas_call(
        functools.partial(middle_kernel, ranks, ky_count),
        in_specs=[VMEM] * 5,
        out_specs=[VMEM] * 3,
        out_shape=[jax.ShapeDtypeStruct(spec.shape, F32), halo, halo],
        scratch_shapes=[
            pltpu.VMEM(spec.shape, F32),
            pltpu.VMEM(spec.shape, F32),
            dma((2,)), dma((ranks,)), dma((ranks,)), dma((ranks,)), dma((ranks,)),
            dma((2,)), dma((2,)),
        ],
        compiler_params=params(collective_id=0, has_side_effects=True),
        name="middle",
    )(spec, pv, green, across, back)


def total_kernel(ranks, x_ref, out_ref, slots, local_sem, send_sem, recv_sem):
    me = lax.axis_index("gx")
    greet(ranks, me)
    wait = exchange(
        ranks, me, lambda d: x_ref, lambda d: slots.at[d], local_sem.at[0], send_sem, recv_sem
    )
    wait()
    out_ref[...] = jnp.sum(slots[...], axis=0)


def total(x, ranks):
    dma = pltpu.SemaphoreType.DMA
    return pl.pallas_call(
        functools.partial(total_kernel, ranks),
        in_specs=[VMEM],
        out_specs=VMEM,
        out_shape=jax.ShapeDtypeStruct(x.shape, F32),
        scratch_shapes=[
            pltpu.VMEM((ranks,) + x.shape, F32), dma((1,)), dma((ranks,)), dma((ranks,)),
        ],
        compiler_params=params(collective_id=1, has_side_effects=True),
        name="total",
    )(x)


def per_device(positions, field, inv_polar, x_spline, yz_spline, tile_list, tile_count):
    ranks = lax.axis_size("gx")
    rank_index = lax.axis_index("gx")
    atoms_here = positions.shape[1]
    planes = GRID // ranks
    extent = planes + 4
    blocks = atoms_here // TILE
    reach = 2 * HALO_BLK + 1
    ky_count = GRID // ranks

    def blocked(x):
        return x.reshape(-1, blocks, TILE).transpose(1, 0, 2)

    all_freq = jnp.arange(GRID, dtype=jnp.int32)
    fourier_rows = basis_rows(GRID, all_freq)
    ky_freq = rank_index * ky_count + jnp.arange(ky_count, dtype=jnp.int32)
    full_modes, full_weights = mode_of(all_freq, GRID)
    ky_modes, ky_weights = mode_of(ky_freq, GRID)
    green = kernel_block(ky_modes, ky_weights, full_modes, full_weights, full_modes, full_weights)
    source_rows = jnp.arange(ranks * extent, dtype=jnp.int32)
    points = (source_rows // extent * planes - 2 + source_rows % extent) % GRID
    across = basis_rows(GRID, points)
    back = across.T
    slots = jnp.arange(tile_list.shape[1], dtype=jnp.int32)
    wanted = jnp.arange(blocks, dtype=jnp.int32)[:, None] + jnp.arange(reach, dtype=jnp.int32)
    live = (slots[None, :] < tile_count[:, None])[:, :, None]
    near = jnp.any((tile_list[:, :, None] == wanted[:, None, :]) & live, axis=1)
    near = near.astype(jnp.int32).reshape(-1)
    yft, zf, zft = prepare(yz_spline, fourier_rows, blocks)
    xs = blocked(x_spline.reshape(2 * ORDER, atoms_here))
    pos = blocked(positions)
    polar = inv_polar.reshape(blocks, 1, TILE)
    spec_shape = jax.ShapeDtypeStruct((ranks, extent, 8, GRID), F32)
    rows_shape = jax.ShapeDtypeStruct((blocks, 3, TILE), F32)

    def apply(vector):
        pv = jnp.concatenate([pos, vector, jnp.zeros((blocks, 2, TILE), F32)], axis=1)
        spec = pl.pallas_call(
            functools.partial(spread_kernel, planes, ky_count),
            in_specs=[VMEM] * 4,
            out_specs=VMEM,
            out_shape=spec_shape,
            compiler_params=params(),
            name="spread",
        )(pv, xs, yft, zf)
        ret, before, after = middle(spec, pv, green, across, back, ranks, ky_count)
        pair = pl.pallas_call(
            pair_kernel,
            in_specs=[pl.BlockSpec(memory_space=pltpu.SMEM)] + [VMEM] * 3,
            out_specs=VMEM,
            out_shape=rows_shape,
            scratch_shapes=[
                pltpu.VMEM((blocks + 2 * HALO_BLK, 8, TILE), F32),
                pltpu.VMEM((6, TILE, TILE), F32),
                pltpu.VMEM((blocks, 3, 8, TILE), F32),
            ],
            compiler_params=params(),
            name="pair",
        )(near, pv, before, after)
        far = pl.pallas_call(
            functools.partial(gather_kernel, planes, ky_count),
            in_specs=[VMEM] * 4,
            out_specs=VMEM,
            out_shape=rows_shape,
            scratch_shapes=[
                pltpu.VMEM((extent, GRID, 2 * GRID), BF16),
                pltpu.VMEM((extent, GRID, GRID), BF16),
            ],
            compiler_params=params(),
            name="gather",
        )(ret, xs, yft, zft)
        return polar * vector + far - pair

    def paired(residual, precond, applied):
        first = jnp.sum(residual * precond, axis=(0, 1))
        second = jnp.sum(applied * precond, axis=(0, 1))
        sums = total(jnp.stack([first, second] + [jnp.zeros_like(first)] * 6), ranks)
        sums = jnp.sum(sums, axis=1)
        return sums[0], sums[1]

    residual = blocked(field)
    dipoles = jnp.zeros_like(residual)
    precond = residual / polar
    applied = apply(precond)
    rz_now, curvature = paired(residual, precond, applied)
    step_size = rz_now / curvature
    direction = precond
    applied_dir = applied
    for sweep_index in range(ITERS):
        dipoles = dipoles + step_size * direction
        residual = residual - step_size * applied_dir
        if sweep_index + 1 < ITERS:
            precond = residual / polar
            applied = apply(precond)
            rz_next, curvature = paired(residual, precond, applied)
            beta_ratio = rz_next / rz_now
            step_size = rz_next / (curvature - beta_ratio * rz_next / step_size)
            direction = precond + beta_ratio * direction
            applied_dir = applied + beta_ratio * applied_dir
            rz_now = rz_next

    def flat(x):
        return x.transpose(1, 0, 2).reshape(3, atoms_here)

    return flat(dipoles), flat(residual)


def solution(mesh):
    placed = (
        P(None, ("rep", "gx")),
        P(None, ("rep", "gx")),
        P(("rep", "gx")),
        P(None, None, ("rep", "gx")),
        P(None, ("rep", "gx"), None),
        P(("rep", "gx"), None),
        P(("rep", "gx")),
    )
    return jax.shard_map(
        per_device,
        mesh=mesh,
        in_specs=placed,
        out_specs=(P(None, ("rep", "gx")), P(None, ("rep", "gx"))),
        check_vma=False,
    )
```

```python
import jax
import jax.numpy as jnp
from jax import lax
from jax.experimental import pallas as pl
from jax.experimental.pallas import tpu as pltpu
from jax.sharding import PartitionSpec as P
import functools
import numpy as np

GRID = 128
ORDER = 5
TILE = 128
HALO_BLK = 3
ITERS = 3


PAIR_C = 0.025
RECIP_C = 8192.0
DAMP = 0.0008
EXACT = lax.Precision.HIGHEST


def mode_of(freq, size):
    half_size = size // 2
    mode_num = jnp.where(freq <= half_size, freq, freq - half_size)
    weight = jnp.where((freq == 0) | (freq == half_size), 1.0 / size, 2.0 / size)
    return (mode_num.astype(jnp.float32), weight.astype(jnp.float32))


def basis_rows(size, points):
    freq = jnp.arange(size, dtype=jnp.int32)
    half_size = size // 2
    mode_num = jnp.where(freq <= half_size, freq, freq - half_size)
    phase = mode_num[:, None] * points[None, :] % size
    angle = phase.astype(jnp.float32) * (2.0 * jnp.pi / size)
    return jnp.where((freq <= half_size)[:, None], jnp.cos(angle), jnp.sin(angle))


def kernel_block(x_modes, x_weights, y_modes, y_weights, z_modes, z_weights):
    mode_sq = (
        x_modes[:, None, None] * x_modes[:, None, None]
        + y_modes[None, :, None] * y_modes[None, :, None]
        + z_modes[None, None, :] * z_modes[None, None, :]
    )
    safe_sq = jnp.where(mode_sq > 0, mode_sq, 1.0)
    green = jnp.where(mode_sq > 0, RECIP_C * jnp.exp(-DAMP * safe_sq) / safe_sq, 0.0)
    return green * x_weights[:, None, None] * y_weights[None, :, None] * z_weights[None, None, :]


F32 = jnp.float32
BF16 = jnp.bfloat16
VMEM = pl.BlockSpec(memory_space=pltpu.VMEM)


def split(x):
    high = x.astype(BF16)
    return high, (x - high.astype(F32)).astype(BF16)


def dot(a, b):
    return jnp.dot(a, b, preferred_element_type=F32)


def params(**more):
    return pltpu.CompilerParams(vmem_limit_bytes=56 * 1024 * 1024, **more)


def prep_kernel(yz_ref, rows_ref, yft_ref, zf_ref, zft_ref):
    rows = jnp.concatenate(split(rows_ref[...]), axis=0)

    def transformed(t):
        high, low = split(jnp.concatenate([yz_ref[t], yz_ref[t + 1]], axis=0))
        contract = (((1,), (1,)), ((), ()))
        wide = lax.dot_general(rows, high, contract, preferred_element_type=F32)
        more = lax.dot_general(rows[:GRID], low, contract, preferred_element_type=F32)
        return wide[:GRID] + wide[GRID:] + more

    lines = transformed(0)
    yft_ref[0, 0] = lines[:, :TILE]
    yft_ref[0, 1] = lines[:, TILE:]
    lines = transformed(2)
    zft_ref[0] = jnp.concatenate(split(lines), axis=0)
    zf_ref[0] = jnp.concatenate(split(lines.T), axis=1)


def prepare(yz_spline, rows, blocks):
    return pl.pallas_call(
        prep_kernel,
        grid=(blocks,),
        in_specs=[
            pl.BlockSpec((4, TILE, GRID), lambda b: (0, b, 0)),
            pl.BlockSpec((GRID, GRID), lambda b: (0, 0)),
        ],
        out_specs=[
            pl.BlockSpec((1, 2, GRID, TILE), lambda b: (b, 0, 0, 0)),
            pl.BlockSpec((1, 2 * TILE, 2 * GRID), lambda b: (b, 0, 0)),
            pl.BlockSpec((1, 2 * GRID, 2 * TILE), lambda b: (b, 0, 0)),
        ],
        out_shape=[
            jax.ShapeDtypeStruct((blocks, 2, GRID, TILE), F32),
            jax.ShapeDtypeStruct((blocks, 2 * TILE, 2 * GRID), BF16),
            jax.ShapeDtypeStruct((blocks, 2 * GRID, 2 * TILE), BF16),
        ],
        compiler_params=params(),
        name="prep",
    )(yz_spline, rows)


def spread_kernel(planes, ky_count, pv_ref, xs_ref, yft_ref, zf_ref, out_ref):
    blocks = pv_ref.shape[0]
    ranks = out_ref.shape[0]
    out_ref[...] = jnp.zeros_like(out_ref)

    def one_block(b, carry):
        base = b * planes // blocks
        y, dy = yft_ref[b, 0], yft_ref[b, 1]
        v0, v1, v2 = (pv_ref[b, 3 + c : 4 + c, :] for c in range(3))
        highs, lows = [], []
        for k in range(ORDER):
            x, dx = xs_ref[b, k : k + 1, :], xs_ref[b, ORDER + k : ORDER + k + 1, :]
            lead = (v0 * dx) * y + (v1 * x) * dy
            high, low = split(jnp.concatenate([lead, (v2 * x) * y], axis=1))
            highs.append(high)
            lows.append(low)
        weights = zf_ref[b]
        wide = dot(jnp.concatenate(highs, axis=0), weights)
        total = (
            wide[:, :GRID] + wide[:, GRID:] + dot(jnp.concatenate(lows, axis=0), weights[:, :GRID])
        )
        for k in range(ORDER):
            part = total[k * GRID : (k + 1) * GRID].reshape(ranks, ky_count, GRID)
            out_ref[:, base + k, :ky_count, :] += part
        return carry

    lax.fori_loop(0, blocks, one_block, 0)


def gather_kernel(
    planes, ky_count, ret_ref, xs_ref, yft_ref, zft_ref, pair_ref, pv_ref, polar_ref,
    next_ref, pv_next_ref, wide_ref, low_ref,
):
    blocks = xs_ref.shape[0]
    extent = ret_ref.shape[1]
    for p in range(extent):
        high, low = split(ret_ref[:, p, :ky_count, :].reshape(GRID, GRID))
        wide_ref[p] = jnp.concatenate([high, high], axis=1)
        low_ref[p] = low

    def one_block(b, carry):
        base = b * planes // blocks
        weights = zft_ref[b]
        wide = wide_ref[pl.ds(base, ORDER)].reshape(ORDER * GRID, 2 * GRID)
        low = low_ref[pl.ds(base, ORDER)].reshape(ORDER * GRID, GRID)
        sums = dot(wide, weights) + dot(low, weights[:GRID])
        one = two = three = 0.0
        for k in range(ORDER):
            x, dx = xs_ref[b, k : k + 1, :], xs_ref[b, ORDER + k : ORDER + k + 1, :]
            plain = sums[k * GRID : (k + 1) * GRID, :TILE]
            one += dx * plain
            two += x * plain
            three += x * sums[k * GRID : (k + 1) * GRID, TILE:]
        y, dy = yft_ref[b, 0], yft_ref[b, 1]
        far = jnp.concatenate(
            [jnp.sum(t, axis=0, keepdims=True) for t in (y * one, dy * two, y * three)], axis=0
        )
        following = pair_ref[b] - far
        next_ref[b] = following
        pv_next_ref[b, 0:3] = pv_ref[b, 0:3]
        pv_next_ref[b, 3:6] = following / polar_ref[b]
        pv_next_ref[b, 6:8] = jnp.zeros((2, TILE), F32)
        return carry

    lax.fori_loop(0, blocks, one_block, 0)


def pair_kernel(near_ref, pv_ref, before_ref, after_ref, out_ref, ext_ref, col_ref, acc_ref):
    blocks = pv_ref.shape[0]
    ext_blocks = ext_ref.shape[0]
    reach = 2 * HALO_BLK + 1
    first_row = lax.broadcasted_iota(jnp.int32, (HALO_BLK, 8, TILE), 1) == 0
    ext_ref[:HALO_BLK] = before_ref[...] + jnp.where(first_row, -1.0 * blocks, 0.0)
    ext_ref[HALO_BLK : HALO_BLK + blocks] = pv_ref[...]
    ext_ref[HALO_BLK + blocks :] = after_ref[...] + jnp.where(first_row, 1.0 * blocks, 0.0)
    acc_ref[...] = jnp.zeros_like(acc_ref)
    lag = lax.broadcasted_iota(jnp.int32, (8, TILE), 1) - lax.broadcasted_iota(
        jnp.int32, (8, TILE), 0
    )

    def one_source(e, carry):
        for c in range(6):
            col_ref[c] = jnp.broadcast_to(ext_ref[e, c : c + 1, :], (TILE, TILE)).T

        def one_home(b, inner):
            @pl.when(near_ref[b * reach + e - b] > 0)
            def _():
                home = [jnp.broadcast_to(pv_ref[b, c : c + 1, :], (8, TILE)) for c in range(3)]
                shift = jnp.where(e == b + HALO_BLK, 0, 4 * TILE)
                direct = [jnp.zeros((8, TILE), F32) for c in range(3)]
                tilted = [jnp.zeros((8, TILE), F32) for c in range(3)]
                for j in range(TILE // 8):
                    rows = slice(8 * j, 8 * j + 8)
                    r = [home[c] - col_ref[c, rows, :] for c in range(3)]
                    v = [col_ref[3 + c, rows, :] for c in range(3)]
                    inverse = lax.rsqrt(r[0] * r[0] + r[1] * r[1] + r[2] * r[2] + 1.0)
                    inverse = jnp.where(lag != 8 * j + shift, inverse, 0.0)
                    square = inverse * inverse
                    third = square * inverse
                    weight = third * square * (r[0] * v[0] + r[1] * v[1] + r[2] * v[2])
                    for c in range(3):
                        direct[c] += third * v[c]
                        tilted[c] += weight * r[c]
                for c in range(3):
                    acc_ref[b, c] += direct[c] - 3.0 * tilted[c]

            return inner

        lo = jnp.maximum(e - (reach - 1), 0)
        hi = jnp.minimum(e + 1, blocks)
        lax.fori_loop(lo, hi, one_home, 0)
        return carry

    lax.fori_loop(0, ext_blocks, one_source, 0)
    for b in range(blocks):
        for c in range(3):
            out_ref[b, c : c + 1] = PAIR_C * jnp.sum(acc_ref[b, c], axis=0, keepdims=True)


def greet(ranks, me):
    barrier = pltpu.get_barrier_semaphore()

    def signal(d, carry):
        pl.semaphore_signal(
            barrier,
            inc=1,
            device_id={"gx": lax.rem(me + d, ranks)},
            device_id_type=pl.DeviceIdType.MESH,
        )
        return carry

    lax.fori_loop(1, ranks, signal, 0)
    pl.semaphore_wait(barrier, ranks - 1)


def exchange(ranks, me, source, target, local_sem, send_sem, recv_sem):
    def copy(d, slot):
        peer = lax.rem(me + d, ranks)
        return pltpu.make_async_remote_copy(
            src_ref=source(peer),
            dst_ref=target(slot),
            send_sem=send_sem.at[d],
            recv_sem=recv_sem.at[d],
            device_id={"gx": peer},
            device_id_type=pl.DeviceIdType.MESH,
        )

    def start(d, carry):
        copy(d, me).start()
        return carry

    def finish(d, carry):
        copy(d, lax.rem(me - d + ranks, ranks)).wait()
        return carry

    lax.fori_loop(1, ranks, start, 0)
    own = pltpu.make_async_copy(source(me), target(me), local_sem)
    own.start()

    def wait():
        own.wait()
        lax.fori_loop(1, ranks, finish, 0)

    return wait


def middle_kernel(
    ranks, ky_count, spec_ref, pv_ref, green_ref, across_ref, back_ref,
    ret_ref, before_ref, after_ref,
    recv_ref, done_ref, local_sems, send1, recv1, send2, recv2, halo_send, halo_recv,
):
    me = lax.axis_index("gx")
    blocks = pv_ref.shape[0]
    extent = spec_ref.shape[1]
    rows = ranks * extent
    greet(ranks, me)
    halos = []
    for t, (piece, into, step) in enumerate(
        (
            (pv_ref.at[pl.ds(blocks - HALO_BLK, HALO_BLK)], before_ref, 1),
            (pv_ref.at[pl.ds(0, HALO_BLK)], after_ref, ranks - 1),
        )
    ):
        halos.append(
            pltpu.make_async_remote_copy(
                src_ref=piece,
                dst_ref=into,
                send_sem=halo_send.at[t],
                recv_sem=halo_recv.at[t],
                device_id={"gx": lax.rem(me + step, ranks)},
                device_id_type=pl.DeviceIdType.MESH,
            )
        )
        halos[-1].start()
    wait = exchange(
        ranks, me, lambda d: spec_ref.at[d], lambda d: recv_ref.at[d], local_sems.at[0], send1, recv1
    )
    across_high, across_low = split(across_ref[...])
    back_high, back_low = split(back_ref[...])
    wait()
    lines_in = recv_ref.reshape(rows * 8, GRID)
    lines_out = done_ref.reshape(rows * 8, GRID)
    for q in range(ky_count):
        high, low = split(lines_in[pl.ds(q, rows, stride=8), :])
        wide = dot(across_high, jnp.concatenate([high, low], axis=1))
        line = wide[:, :GRID] + wide[:, GRID:] + dot(across_low, high)
        high, low = split(line * green_ref[q])
        wide = dot(back_high, jnp.concatenate([high, low], axis=1))
        lines_out[pl.ds(q, rows, stride=8), :] = (
            wide[:, :GRID] + wide[:, GRID:] + dot(back_low, high)
        )
    wait = exchange(
        ranks, me, lambda d: done_ref.at[d], lambda d: ret_ref.at[d], local_sems.at[1], send2, recv2
    )
    for halo in halos:
        halo.wait()
    wait()


def middle(spec, pv, green, across, back, ranks, ky_count):
    dma = pltpu.SemaphoreType.DMA
    halo = jax.ShapeDtypeStruct((HALO_BLK, 8, TILE), F32)
    return pl.pallas_call(
        functools.partial(middle_kernel, ranks, ky_count),
        in_specs=[VMEM] * 5,
        out_specs=[VMEM] * 3,
        out_shape=[jax.ShapeDtypeStruct(spec.shape, F32), halo, halo],
        scratch_shapes=[
            pltpu.VMEM(spec.shape, F32),
            pltpu.VMEM(spec.shape, F32),
            dma((2,)), dma((ranks,)), dma((ranks,)), dma((ranks,)), dma((ranks,)),
            dma((2,)), dma((2,)),
        ],
        compiler_params=params(collective_id=0, has_side_effects=True),
        name="middle",
    )(spec, pv, green, across, back)


def combine(weights, parts):
    terms = [w * p for w, p in zip(weights, parts) if w is not None]
    return functools.reduce(jnp.add, terms)


def scaled(a, x, y):
    pairs = zip(x, y)
    return [p if q is None else (a * q if p is None else p + a * q) for p, q in pairs]


def solve_kernel(
    ranks, b0_ref, b1_ref, b2_ref, b3_ref, polar_ref,
    dipoles_ref, residual_ref, part_ref, slots, local_sem, send_sem, recv_sem,
):
    me = lax.axis_index("gx")
    bases = [ref[...] for ref in (b0_ref, b1_ref, b2_ref, b3_ref)]
    soft = [b / polar_ref[...] for b in bases]
    count = ITERS + 1
    place = {}
    part_ref[...] = jnp.zeros_like(part_ref)
    for i in range(count):
        for j in range(i, count):
            place[i, j] = place[j, i] = row = len(set(place.values()))
            part_ref[row : row + 1] = jnp.sum(
                jnp.sum(bases[i] * soft[j], axis=0), axis=0, keepdims=True
            )
    greet(ranks, me)
    wait = exchange(
        ranks, me, lambda d: part_ref, lambda d: slots.at[d], local_sem.at[0], send_sem, recv_sem
    )
    wait()
    sums = jnp.sum(jnp.sum(slots[...], axis=0), axis=1, keepdims=True)
    sums = jnp.broadcast_to(sums, (sums.shape[0], TILE))

    def inner(x, y):
        value = None
        for i in range(count):
            for j in range(count):
                if x[i] is not None and y[j] is not None:
                    row = place[i, j]
                    term = x[i] * y[j] * sums[row : row + 1]
                    value = term if value is None else value + term
        return value

    none = [None] * (count - 1)
    residual = [jnp.ones((1, TILE), F32)] + none
    direction = list(residual)
    dipoles = [None] * count
    rz_now = inner(residual, residual)
    for sweep in range(ITERS):
        image = scaled(-1.0, direction, [None] + direction[:-1])
        step = rz_now / inner(direction, image)
        dipoles = scaled(step, dipoles, direction)
        residual = scaled(-step, residual, image)
        if sweep + 1 < ITERS:
            rz_next = inner(residual, residual)
            direction = scaled(rz_next / rz_now, residual, direction)
            rz_now = rz_next
    dipoles_ref[...] = combine(dipoles, soft)
    residual_ref[...] = combine(residual, bases)


def solve(bases, polar, ranks):
    dma = pltpu.SemaphoreType.DMA
    shape = bases[0].shape
    return pl.pallas_call(
        functools.partial(solve_kernel, ranks),
        in_specs=[VMEM] * 5,
        out_specs=[VMEM] * 2,
        out_shape=[jax.ShapeDtypeStruct(shape, F32)] * 2,
        scratch_shapes=[
            pltpu.VMEM((16, TILE), F32), pltpu.VMEM((ranks, 16, TILE), F32),
            dma((1,)), dma((ranks,)), dma((ranks,)),
        ],
        compiler_params=params(collective_id=1, has_side_effects=True),
        name="solve",
    )(*bases, polar)


def fixed_rows(points):
    half_size = GRID // 2
    freq = np.arange(GRID)
    mode_num = np.where(freq <= half_size, freq, freq - half_size)
    angle = (mode_num[:, None] * points[None, :] % GRID) * (2.0 * np.pi / GRID)
    return np.where((freq <= half_size)[:, None], np.cos(angle), np.sin(angle)).astype(np.float32)


def per_device(positions, field, inv_polar, x_spline, yz_spline, tile_list, tile_count):
    ranks = lax.axis_size("gx")
    rank_index = lax.axis_index("gx")
    atoms_here = positions.shape[1]
    planes = GRID // ranks
    extent = planes + 4
    blocks = atoms_here // TILE
    reach = 2 * HALO_BLK + 1
    ky_count = GRID // ranks

    def blocked(x):
        return x.reshape(-1, blocks, TILE).transpose(1, 0, 2)

    all_freq = jnp.arange(GRID, dtype=jnp.int32)
    fourier_rows = jnp.asarray(fixed_rows(np.arange(GRID)))
    ky_freq = rank_index * ky_count + jnp.arange(ky_count, dtype=jnp.int32)
    full_modes, full_weights = mode_of(all_freq, GRID)
    ky_modes, ky_weights = mode_of(ky_freq, GRID)
    green = kernel_block(ky_modes, ky_weights, full_modes, full_weights, full_modes, full_weights)
    source_rows = np.arange(ranks * extent)
    points = (source_rows // extent * planes - 2 + source_rows % extent) % GRID
    across = fixed_rows(points)
    back = jnp.asarray(np.ascontiguousarray(across.T))
    across = jnp.asarray(across)
    slots = jnp.arange(tile_list.shape[1], dtype=jnp.int32)
    wanted = jnp.arange(blocks, dtype=jnp.int32)[:, None] + jnp.arange(reach, dtype=jnp.int32)
    live = (slots[None, :] < tile_count[:, None])[:, :, None]
    near = jnp.any((tile_list[:, :, None] == wanted[:, None, :]) & live, axis=1)
    near = near.astype(jnp.int32).reshape(-1)
    yft, zf, zft = prepare(yz_spline, fourier_rows, blocks)
    xs = blocked(x_spline.reshape(2 * ORDER, atoms_here))
    pos = blocked(positions)
    polar = inv_polar.reshape(blocks, 1, TILE)
    spec_shape = jax.ShapeDtypeStruct((ranks, extent, 8, GRID), F32)
    rows_shape = jax.ShapeDtypeStruct((blocks, 3, TILE), F32)

    def advance(pv):
        spec = pl.pallas_call(
            functools.partial(spread_kernel, planes, ky_count),
            in_specs=[VMEM] * 4,
            out_specs=VMEM,
            out_shape=spec_shape,
            compiler_params=params(),
            name="spread",
        )(pv, xs, yft, zf)
        ret, before, after = middle(spec, pv, green, across, back, ranks, ky_count)
        pair = pl.pallas_call(
            pair_kernel,
            in_specs=[pl.BlockSpec(memory_space=pltpu.SMEM)] + [VMEM] * 3,
            out_specs=VMEM,
            out_shape=rows_shape,
            scratch_shapes=[
                pltpu.VMEM((blocks + 2 * HALO_BLK, 8, TILE), F32),
                pltpu.VMEM((6, TILE, TILE), F32),
                pltpu.VMEM((blocks, 3, 8, TILE), F32),
            ],
            compiler_params=params(),
            name="pair",
        )(near, pv, before, after)
        return pl.pallas_call(
            functools.partial(gather_kernel, planes, ky_count),
            in_specs=[VMEM] * 7,
            out_specs=[VMEM] * 2,
            out_shape=[rows_shape, jax.ShapeDtypeStruct((blocks, 8, TILE), F32)],
            scratch_shapes=[
                pltpu.VMEM((extent, GRID, 2 * GRID), BF16),
                pltpu.VMEM((extent, GRID, GRID), BF16),
            ],
            compiler_params=params(),
            name="gather",
        )(ret, xs, yft, zft, pair, pv, polar)

    bases = [blocked(field)]
    pv = jnp.concatenate([pos, bases[0] / polar, jnp.zeros((blocks, 2, TILE), F32)], axis=1)
    for sweep in range(ITERS):
        following, pv = advance(pv)
        bases.append(following)
    dipoles, residual = solve(bases, polar, ranks)

    def flat(x):
        return x.transpose(1, 0, 2).reshape(3, atoms_here)

    return flat(dipoles), flat(residual)


def solution(mesh):
    placed = (
        P(None, ("rep", "gx")),
        P(None, ("rep", "gx")),
        P(("rep", "gx")),
        P(None, None, ("rep", "gx")),
        P(None, ("rep", "gx"), None),
        P(("rep", "gx"), None),
        P(("rep", "gx")),
    )
    return jax.shard_map(
        per_device,
        mesh=mesh,
        in_specs=placed,
        out_specs=(P(None, ("rep", "gx")), P(None, ("rep", "gx"))),
        check_vma=False,
    )
```

```python
import jax
import jax.numpy as jnp
from jax import lax
from jax.experimental import pallas as pl
from jax.experimental.pallas import tpu as pltpu
from jax.sharding import PartitionSpec as P
import functools
import numpy as np

GRID = 128
ORDER = 5
TILE = 128
HALO_BLK = 3
ITERS = 3


PAIR_C = 0.025
RECIP_C = 8192.0
DAMP = 0.0008
EXACT = lax.Precision.HIGHEST


def mode_of(freq, size):
    half_size = size // 2
    mode_num = jnp.where(freq <= half_size, freq, freq - half_size)
    weight = jnp.where((freq == 0) | (freq == half_size), 1.0 / size, 2.0 / size)
    return (mode_num.astype(jnp.float32), weight.astype(jnp.float32))


def basis_rows(size, points):
    freq = jnp.arange(size, dtype=jnp.int32)
    half_size = size // 2
    mode_num = jnp.where(freq <= half_size, freq, freq - half_size)
    phase = mode_num[:, None] * points[None, :] % size
    angle = phase.astype(jnp.float32) * (2.0 * jnp.pi / size)
    return jnp.where((freq <= half_size)[:, None], jnp.cos(angle), jnp.sin(angle))


def kernel_block(x_modes, x_weights, y_modes, y_weights, z_modes, z_weights):
    mode_sq = (
        x_modes[:, None, None] * x_modes[:, None, None]
        + y_modes[None, :, None] * y_modes[None, :, None]
        + z_modes[None, None, :] * z_modes[None, None, :]
    )
    safe_sq = jnp.where(mode_sq > 0, mode_sq, 1.0)
    green = jnp.where(mode_sq > 0, RECIP_C * jnp.exp(-DAMP * safe_sq) / safe_sq, 0.0)
    return green * x_weights[:, None, None] * y_weights[None, :, None] * z_weights[None, None, :]


F32 = jnp.float32
BF16 = jnp.bfloat16
VMEM = pl.BlockSpec(memory_space=pltpu.VMEM)


def split(x):
    high = x.astype(BF16)
    return high, (x - high.astype(F32)).astype(BF16)


def dot(a, b):
    return jnp.dot(a, b, preferred_element_type=F32)


def params(**more):
    return pltpu.CompilerParams(vmem_limit_bytes=56 * 1024 * 1024, **more)


def prep_kernel(yz_ref, rows_ref, yft_ref, zf_ref, zft_ref):
    rows = jnp.concatenate(split(rows_ref[...]), axis=0)

    def transformed(t):
        high, low = split(jnp.concatenate([yz_ref[t], yz_ref[t + 1]], axis=0))
        contract = (((1,), (1,)), ((), ()))
        wide = lax.dot_general(rows, high, contract, preferred_element_type=F32)
        more = lax.dot_general(rows[:GRID], low, contract, preferred_element_type=F32)
        return wide[:GRID] + wide[GRID:] + more

    lines = transformed(0)
    yft_ref[0, 0] = lines[:, :TILE]
    yft_ref[0, 1] = lines[:, TILE:]
    lines = transformed(2)
    zft_ref[0] = jnp.concatenate(split(lines), axis=0)
    zf_ref[0] = jnp.concatenate(split(lines.T), axis=1)


def prepare(yz_spline, rows, blocks):
    return pl.pallas_call(
        prep_kernel,
        grid=(blocks,),
        in_specs=[
            pl.BlockSpec((4, TILE, GRID), lambda b: (0, b, 0)),
            pl.BlockSpec((GRID, GRID), lambda b: (0, 0)),
        ],
        out_specs=[
            pl.BlockSpec((1, 2, GRID, TILE), lambda b: (b, 0, 0, 0)),
            pl.BlockSpec((1, 2 * TILE, 2 * GRID), lambda b: (b, 0, 0)),
            pl.BlockSpec((1, 2 * GRID, 2 * TILE), lambda b: (b, 0, 0)),
        ],
        out_shape=[
            jax.ShapeDtypeStruct((blocks, 2, GRID, TILE), F32),
            jax.ShapeDtypeStruct((blocks, 2 * TILE, 2 * GRID), BF16),
            jax.ShapeDtypeStruct((blocks, 2 * GRID, 2 * TILE), BF16),
        ],
        compiler_params=params(),
        name="prep",
    )(yz_spline, rows)


def spread_kernel(planes, ky_count, pv_ref, xs_ref, yft_ref, zf_ref, out_ref):
    blocks = pv_ref.shape[0]
    ranks = out_ref.shape[0]
    out_ref[...] = jnp.zeros_like(out_ref)

    def one_block(b, carry):
        base = b * planes // blocks
        y, dy = yft_ref[b, 0], yft_ref[b, 1]
        v0, v1, v2 = (pv_ref[b, 3 + c : 4 + c, :] for c in range(3))
        highs, lows = [], []
        for k in range(ORDER):
            x, dx = xs_ref[b, k : k + 1, :], xs_ref[b, ORDER + k : ORDER + k + 1, :]
            lead = (v0 * dx) * y + (v1 * x) * dy
            high, low = split(jnp.concatenate([lead, (v2 * x) * y], axis=1))
            highs.append(high)
            lows.append(low)
        weights = zf_ref[b]
        wide = dot(jnp.concatenate(highs, axis=0), weights)
        total = (
            wide[:, :GRID] + wide[:, GRID:] + dot(jnp.concatenate(lows, axis=0), weights[:, :GRID])
        )
        for k in range(ORDER):
            part = total[k * GRID : (k + 1) * GRID].reshape(ranks, ky_count, GRID)
            out_ref[:, base + k, :ky_count, :] += part
        return carry

    lax.fori_loop(0, blocks, one_block, 0)


def gather_kernel(
    planes, ky_count, ret_ref, xs_ref, yft_ref, zft_ref, pair_ref, pv_ref, polar_ref,
    next_ref, pv_next_ref, wide_ref, low_ref,
):
    blocks = xs_ref.shape[0]
    extent = ret_ref.shape[1]
    for p in range(extent):
        high, low = split(ret_ref[:, p, :ky_count, :].reshape(GRID, GRID))
        wide_ref[p] = jnp.concatenate([high, high], axis=1)
        low_ref[p] = low

    def one_block(b, carry):
        base = b * planes // blocks
        weights = zft_ref[b]
        wide = wide_ref[pl.ds(base, ORDER)].reshape(ORDER * GRID, 2 * GRID)
        low = low_ref[pl.ds(base, ORDER)].reshape(ORDER * GRID, GRID)
        sums = dot(wide, weights) + dot(low, weights[:GRID])
        one = two = three = 0.0
        for k in range(ORDER):
            x, dx = xs_ref[b, k : k + 1, :], xs_ref[b, ORDER + k : ORDER + k + 1, :]
            plain = sums[k * GRID : (k + 1) * GRID, :TILE]
            one += dx * plain
            two += x * plain
            three += x * sums[k * GRID : (k + 1) * GRID, TILE:]
        y, dy = yft_ref[b, 0], yft_ref[b, 1]
        far = jnp.concatenate(
            [jnp.sum(t, axis=0, keepdims=True) for t in (y * one, dy * two, y * three)], axis=0
        )
        following = pair_ref[b] - far
        next_ref[b] = following
        pv_next_ref[b, 0:3] = pv_ref[b, 0:3]
        pv_next_ref[b, 3:6] = following / polar_ref[b]
        pv_next_ref[b, 6:8] = jnp.zeros((2, TILE), F32)
        return carry

    lax.fori_loop(0, blocks, one_block, 0)


def pair_sum(near_ref, pv_ref, before_ref, after_ref, out_ref, ext_ref, col_ref):
    blocks = pv_ref.shape[0]
    reach = 2 * HALO_BLK + 1
    first_row = lax.broadcasted_iota(jnp.int32, (HALO_BLK, 8, TILE), 1) == 0
    ext_ref[:HALO_BLK] = before_ref[...] + jnp.where(first_row, -1.0 * blocks, 0.0)
    ext_ref[HALO_BLK : HALO_BLK + blocks] = pv_ref[...]
    ext_ref[HALO_BLK + blocks :] = after_ref[...] + jnp.where(first_row, 1.0 * blocks, 0.0)
    lag = lax.broadcasted_iota(jnp.int32, (8, TILE), 1) - lax.broadcasted_iota(
        jnp.int32, (8, TILE), 0
    )

    def spread_columns(e, carry):
        for c in range(6):
            col_ref[e, c] = jnp.broadcast_to(ext_ref[e, c : c + 1, :], (TILE, TILE)).T
        return carry

    lax.fori_loop(0, blocks + 2 * HALO_BLK, spread_columns, 0)

    def one_home(b, carry):
        home = [jnp.broadcast_to(pv_ref[b, c : c + 1, :], (8, TILE)) for c in range(3)]

        def one_source(k, sums):
            shift = jnp.where(k == HALO_BLK, 0, 4 * TILE)
            direct = [jnp.zeros((8, TILE), F32) for c in range(3)]
            tilted = [jnp.zeros((8, TILE), F32) for c in range(3)]
            for j in range(TILE // 8):
                rows = slice(8 * j, 8 * j + 8)
                r = [home[c] - col_ref[b + k, c, rows, :] for c in range(3)]
                v = [col_ref[b + k, 3 + c, rows, :] for c in range(3)]
                inverse = lax.rsqrt(r[0] * r[0] + r[1] * r[1] + r[2] * r[2] + 1.0)
                inverse = jnp.where(lag != 8 * j + shift, inverse, 0.0)
                square = inverse * inverse
                third = square * inverse
                weight = third * square * (r[0] * v[0] + r[1] * v[1] + r[2] * v[2])
                for c in range(3):
                    direct[c] += third * v[c]
                    tilted[c] += weight * r[c]
            near = near_ref[b * reach + k]
            return tuple(
                sums[c] + near * (direct[c] - 3.0 * tilted[c]) for c in range(3)
            )

        sums = lax.fori_loop(0, reach, one_source, (jnp.zeros((8, TILE), F32),) * 3)
        out_ref[b] = PAIR_C * jnp.concatenate(
            [jnp.sum(t, axis=0, keepdims=True) for t in sums], axis=0
        )
        return carry

    lax.fori_loop(0, blocks, one_home, 0)


def greet(ranks, me):
    barrier = pltpu.get_barrier_semaphore()

    def signal(d, carry):
        pl.semaphore_signal(
            barrier,
            inc=1,
            device_id={"gx": lax.rem(me + d, ranks)},
            device_id_type=pl.DeviceIdType.MESH,
        )
        return carry

    lax.fori_loop(1, ranks, signal, 0)
    pl.semaphore_wait(barrier, ranks - 1)


def exchange(ranks, me, source, target, local_sem, send_sem, recv_sem):
    def copy(d, slot):
        peer = lax.rem(me + d, ranks)
        return pltpu.make_async_remote_copy(
            src_ref=source(peer),
            dst_ref=target(slot),
            send_sem=send_sem.at[d],
            recv_sem=recv_sem.at[d],
            device_id={"gx": peer},
            device_id_type=pl.DeviceIdType.MESH,
        )

    def start(d, carry):
        copy(d, me).start()
        return carry

    def finish(d, carry):
        copy(d, lax.rem(me - d + ranks, ranks)).wait()
        return carry

    lax.fori_loop(1, ranks, start, 0)
    own = pltpu.make_async_copy(source(me), target(me), local_sem)
    own.start()

    def wait():
        own.wait()
        lax.fori_loop(1, ranks, finish, 0)

    return wait


def middle_kernel(
    ranks, ky_count, near_ref, spec_ref, pv_ref, green_ref, across_ref, back_ref,
    ret_ref, pair_ref,
    before_ref, after_ref, ext_ref, col_ref, recv_ref, done_ref, local_sems, send1, recv1, send2, recv2, halo_send, halo_recv,
):
    me = lax.axis_index("gx")
    blocks = pv_ref.shape[0]
    extent = spec_ref.shape[1]
    rows = ranks * extent
    greet(ranks, me)
    halos = []
    for t, (piece, into, step) in enumerate(
        (
            (pv_ref.at[pl.ds(blocks - HALO_BLK, HALO_BLK)], before_ref, 1),
            (pv_ref.at[pl.ds(0, HALO_BLK)], after_ref, ranks - 1),
        )
    ):
        halos.append(
            pltpu.make_async_remote_copy(
                src_ref=piece,
                dst_ref=into,
                send_sem=halo_send.at[t],
                recv_sem=halo_recv.at[t],
                device_id={"gx": lax.rem(me + step, ranks)},
                device_id_type=pl.DeviceIdType.MESH,
            )
        )
        halos[-1].start()
    wait = exchange(
        ranks, me, lambda d: spec_ref.at[d], lambda d: recv_ref.at[d], local_sems.at[0], send1, recv1
    )
    across_high, across_low = split(across_ref[...])
    back_high, back_low = split(back_ref[...])
    wait()
    lines_in = recv_ref.reshape(rows * 8, GRID)
    lines_out = done_ref.reshape(rows * 8, GRID)
    for q in range(ky_count):
        high, low = split(lines_in[pl.ds(q, rows, stride=8), :])
        wide = dot(across_high, jnp.concatenate([high, low], axis=1))
        line = wide[:, :GRID] + wide[:, GRID:] + dot(across_low, high)
        high, low = split(line * green_ref[q])
        wide = dot(back_high, jnp.concatenate([high, low], axis=1))
        lines_out[pl.ds(q, rows, stride=8), :] = (
            wide[:, :GRID] + wide[:, GRID:] + dot(back_low, high)
        )
    wait = exchange(
        ranks, me, lambda d: done_ref.at[d], lambda d: ret_ref.at[d], local_sems.at[1], send2, recv2
    )
    for halo in halos:
        halo.wait()
    pair_sum(near_ref, pv_ref, before_ref, after_ref, pair_ref, ext_ref, col_ref)
    wait()


def middle(near, spec, pv, green, across, back, ranks, ky_count):
    dma = pltpu.SemaphoreType.DMA
    blocks = pv.shape[0]
    halo = pltpu.VMEM((HALO_BLK, 8, TILE), F32)
    return pl.pallas_call(
        functools.partial(middle_kernel, ranks, ky_count),
        in_specs=[pl.BlockSpec(memory_space=pltpu.SMEM)] + [VMEM] * 5,
        out_specs=[VMEM] * 2,
        out_shape=[
            jax.ShapeDtypeStruct(spec.shape, F32),
            jax.ShapeDtypeStruct((blocks, 3, TILE), F32),
        ],
        scratch_shapes=[
            halo,
            halo,
            pltpu.VMEM((blocks + 2 * HALO_BLK, 8, TILE), F32),
            pltpu.VMEM((blocks + 2 * HALO_BLK, 6, TILE, TILE), F32),
            pltpu.VMEM(spec.shape, F32),
            pltpu.VMEM(spec.shape, F32),
            dma((2,)), dma((ranks,)), dma((ranks,)), dma((ranks,)), dma((ranks,)),
            dma((2,)), dma((2,)),
        ],
        compiler_params=params(collective_id=0, has_side_effects=True),
        name="middle",
    )(near, spec, pv, green, across, back)


def combine(weights, parts):
    terms = [w * p for w, p in zip(weights, parts) if w is not None]
    return functools.reduce(jnp.add, terms)


def scaled(a, x, y):
    pairs = zip(x, y)
    return [p if q is None else (a * q if p is None else p + a * q) for p, q in pairs]


def solve_kernel(
    ranks, b0_ref, b1_ref, b2_ref, b3_ref, polar_ref,
    dipoles_ref, residual_ref, part_ref, slots, local_sem, send_sem, recv_sem,
):
    me = lax.axis_index("gx")
    bases = [ref[...] for ref in (b0_ref, b1_ref, b2_ref, b3_ref)]
    soft = [b / polar_ref[...] for b in bases]
    count = ITERS + 1
    place = {}
    part_ref[...] = jnp.zeros_like(part_ref)
    for i in range(count):
        for j in range(i, count):
            place[i, j] = place[j, i] = row = len(set(place.values()))
            part_ref[row : row + 1] = jnp.sum(
                jnp.sum(bases[i] * soft[j], axis=0), axis=0, keepdims=True
            )
    greet(ranks, me)
    wait = exchange(
        ranks, me, lambda d: part_ref, lambda d: slots.at[d], local_sem.at[0], send_sem, recv_sem
    )
    wait()
    sums = jnp.sum(jnp.sum(slots[...], axis=0), axis=1, keepdims=True)
    sums = jnp.broadcast_to(sums, (sums.shape[0], TILE))

    def inner(x, y):
        value = None
        for i in range(count):
            for j in range(count):
                if x[i] is not None and y[j] is not None:
                    row = place[i, j]
                    term = x[i] * y[j] * sums[row : row + 1]
                    value = term if value is None else value + term
        return value

    none = [None] * (count - 1)
    residual = [jnp.ones((1, TILE), F32)] + none
    direction = list(residual)
    dipoles = [None] * count
    rz_now = inner(residual, residual)
    for sweep in range(ITERS):
        image = scaled(-1.0, direction, [None] + direction[:-1])
        step = rz_now / inner(direction, image)
        dipoles = scaled(step, dipoles, direction)
        residual = scaled(-step, residual, image)
        if sweep + 1 < ITERS:
            rz_next = inner(residual, residual)
            direction = scaled(rz_next / rz_now, residual, direction)
            rz_now = rz_next
    dipoles_ref[...] = combine(dipoles, soft)
    residual_ref[...] = combine(residual, bases)


def solve(bases, polar, ranks):
    dma = pltpu.SemaphoreType.DMA
    shape = bases[0].shape
    return pl.pallas_call(
        functools.partial(solve_kernel, ranks),
        in_specs=[VMEM] * 5,
        out_specs=[VMEM] * 2,
        out_shape=[jax.ShapeDtypeStruct(shape, F32)] * 2,
        scratch_shapes=[
            pltpu.VMEM((16, TILE), F32), pltpu.VMEM((ranks, 16, TILE), F32),
            dma((1,)), dma((ranks,)), dma((ranks,)),
        ],
        compiler_params=params(collective_id=1, has_side_effects=True),
        name="solve",
    )(*bases, polar)


def fixed_rows(points):
    half_size = GRID // 2
    freq = np.arange(GRID)
    mode_num = np.where(freq <= half_size, freq, freq - half_size)
    angle = (mode_num[:, None] * points[None, :] % GRID) * (2.0 * np.pi / GRID)
    return np.where((freq <= half_size)[:, None], np.cos(angle), np.sin(angle)).astype(np.float32)


def per_device(positions, field, inv_polar, x_spline, yz_spline, tile_list, tile_count):
    ranks = lax.axis_size("gx")
    rank_index = lax.axis_index("gx")
    atoms_here = positions.shape[1]
    planes = GRID // ranks
    extent = planes + 4
    blocks = atoms_here // TILE
    reach = 2 * HALO_BLK + 1
    ky_count = GRID // ranks

    def blocked(x):
        return x.reshape(-1, blocks, TILE).transpose(1, 0, 2)

    all_freq = jnp.arange(GRID, dtype=jnp.int32)
    fourier_rows = jnp.asarray(fixed_rows(np.arange(GRID)))
    ky_freq = rank_index * ky_count + jnp.arange(ky_count, dtype=jnp.int32)
    full_modes, full_weights = mode_of(all_freq, GRID)
    ky_modes, ky_weights = mode_of(ky_freq, GRID)
    green = kernel_block(ky_modes, ky_weights, full_modes, full_weights, full_modes, full_weights)
    source_rows = np.arange(ranks * extent)
    points = (source_rows // extent * planes - 2 + source_rows % extent) % GRID
    across = fixed_rows(points)
    back = jnp.asarray(np.ascontiguousarray(across.T))
    across = jnp.asarray(across)
    slots = jnp.arange(tile_list.shape[1], dtype=jnp.int32)
    wanted = jnp.arange(blocks, dtype=jnp.int32)[:, None] + jnp.arange(reach, dtype=jnp.int32)
    live = (slots[None, :] < tile_count[:, None])[:, :, None]
    near = jnp.any((tile_list[:, :, None] == wanted[:, None, :]) & live, axis=1)
    near = near.astype(F32).reshape(-1)
    yft, zf, zft = prepare(yz_spline, fourier_rows, blocks)
    xs = blocked(x_spline.reshape(2 * ORDER, atoms_here))
    pos = blocked(positions)
    polar = inv_polar.reshape(blocks, 1, TILE)
    spec_shape = jax.ShapeDtypeStruct((ranks, extent, 8, GRID), F32)
    rows_shape = jax.ShapeDtypeStruct((blocks, 3, TILE), F32)

    def advance(pv):
        spec = pl.pallas_call(
            functools.partial(spread_kernel, planes, ky_count),
            in_specs=[VMEM] * 4,
            out_specs=VMEM,
            out_shape=spec_shape,
            compiler_params=params(),
            name="spread",
        )(pv, xs, yft, zf)
        ret, pair = middle(near, spec, pv, green, across, back, ranks, ky_count)
        return pl.pallas_call(
            functools.partial(gather_kernel, planes, ky_count),
            in_specs=[VMEM] * 7,
            out_specs=[VMEM] * 2,
            out_shape=[rows_shape, jax.ShapeDtypeStruct((blocks, 8, TILE), F32)],
            scratch_shapes=[
                pltpu.VMEM((extent, GRID, 2 * GRID), BF16),
                pltpu.VMEM((extent, GRID, GRID), BF16),
            ],
            compiler_params=params(),
            name="gather",
        )(ret, xs, yft, zft, pair, pv, polar)

    bases = [blocked(field)]
    pv = jnp.concatenate([pos, bases[0] / polar, jnp.zeros((blocks, 2, TILE), F32)], axis=1)
    for sweep in range(ITERS):
        following, pv = advance(pv)
        bases.append(following)
    dipoles, residual = solve(bases, polar, ranks)

    def flat(x):
        return x.transpose(1, 0, 2).reshape(3, atoms_here)

    return flat(dipoles), flat(residual)


def solution(mesh):
    placed = (
        P(None, ("rep", "gx")),
        P(None, ("rep", "gx")),
        P(("rep", "gx")),
        P(None, None, ("rep", "gx")),
        P(None, ("rep", "gx"), None),
        P(("rep", "gx"), None),
        P(("rep", "gx")),
    )
    return jax.shard_map(
        per_device,
        mesh=mesh,
        in_specs=placed,
        out_specs=(P(None, ("rep", "gx")), P(None, ("rep", "gx"))),
        check_vma=False,
    )
```
